32 devices in a mesh: grp: 4 (over x, core), ep: 4 (over z), sq: 2 (over y).
Axes of the slice: x: 2, y: 2, z: 4, core: 2. Of those that a mesh axis runs over, the one named last changes fastest.
Arguments:
- queries: bfloat16 [8192, 2048], P(('grp', 'ep', 'sq')), may hold values from -32 to 32
- keys: bfloat16 [8192, 512], P(('grp', 'ep', 'sq')), may hold values from -32 to 32
- values: bfloat16 [8192, 512], P(('grp', 'ep', 'sq')), may hold values from -6 to 6
- norm_gain: float32 [2048], replicated, may hold values from 0.1 to 1.9
- expert_ids: int32 [8192, 2], P(('grp', 'ep', 'sq')), may hold values from 0 to 3, all different within a row; in each aligned block of 256 rows (0 to 255, 256 to 511, ...) at most 192 rows name the same one
- gate_values: float32 [8192, 2], P(('grp', 'ep', 'sq')), may hold values from 0.1 to 1
- hidden_grad: bfloat16 [8192, 1024], P(('grp', 'ep', 'sq')), may hold values from -0.59765625 to 0.59765625
- gate_weight: bfloat16 [4, 2048, 1024], P('ep', None, 'sq'), may hold values from -0.125 to 0.125
- up_weight: bfloat16 [4, 2048, 1024], P('ep', None, 'sq'), may hold values from -0.125 to 0.125
Outputs:
- gate_grad: float32 [4, 2048, 1024], P('ep', 'grp', 'sq')
The draws below stay inside these ranges and needn't reach their ends.
Inputs may be any that keep to these rules, and one draw needn't show every extreme that they name: `expert_ids`: each token names 2 different experts; within the 256 tokens of one device no expert is named more than 192 times.
All inputs are finite; a program needn't handle non-finite values.
Results may differ from the reference program's by a relative error of at most 0.0085.
Values may be sent and summed in bfloat16 or wider, within the bound.
A program may use at most 64 MiB of HBM per device.

```python
import math
import jax
import jax.numpy as jnp
import numpy as np
from jax import lax

D = 2048
HEADS = 16
HEAD_DIM = 128
KV_HEADS = 4
FF = 1024
TOP = 2
LENGTH = 512
TOK_DEV = 256
EXPERTS = 4
CAP = 192
REPLICAS = 4
REPLICA_TOKENS = 2048
TOKENS = 8192
N_EP = 4
N_SQ = 2


def draw_queries(key, part):
    drawn = jnp.clip(jax.random.normal(jax.random.fold_in(key, 11), (TOKENS, HEADS * HEAD_DIM), jnp.float32), -3.5, 3.5)
    return drawn.astype(jnp.bfloat16)


def draw_keys(key, part):
    drawn = jnp.clip(jax.random.normal(jax.random.fold_in(key, 12), (TOKENS, KV_HEADS * HEAD_DIM), jnp.float32), -3.5, 3.5)
    return drawn.astype(jnp.bfloat16)


def block_scale(key, shape, shards, least, high):
    factor_of = 1.0
    for position, blocks in shards:
        draws = jax.random.uniform(jax.random.fold_in(jax.random.fold_in(key, 6), position), (blocks,), jnp.float32, least / len(shards), high / len(shards))
        factor_of = factor_of * jnp.repeat(jnp.exp(draws), shape[position] // blocks).reshape((-1,) + (1,) * (len(shape) - 1 - position))
    return factor_of


def routed_block(key, own, number, rows, amount, top, bound, skew):
    order = jax.random.permutation(key, amount)
    packed, common = portions_of(amount, rows * top, bound, skew, True), portions_of(amount, rows * top, bound, skew, False)
    places = jnp.arange(amount)

    def named(lengths, rotation):
        used = int((lengths > 0).sum())
        fixed = max(1, used // 4)
        moved = fixed + (places - fixed + rotation * (used - fixed)) % max(1, amount - fixed)
        return jnp.zeros((amount,), jnp.int32).at[order[jnp.where(places < fixed, places, moved)]].set(jnp.asarray(lengths, jnp.int32))

    lengths = jnp.where(number % 4 == 0, named(packed, number // 4), named(common, number - number // 4 - 1))
    mixed = jax.random.permutation(jax.random.fold_in(own, 3), amount)
    donor, receiver = mixed[0:amount // 2 * 2:2], mixed[1:amount // 2 * 2:2]
    slack = jnp.minimum(lengths[donor] - 1, bound - lengths[receiver]) // 2
    slack = jnp.where((donor == order[0]) | (receiver == order[0]) | (lengths[receiver] == 0), 0, jnp.maximum(slack, 0))
    moved = jax.random.randint(jax.random.fold_in(own, 4), (amount // 2,), 0, 1 << 20) % (slack + 1)
    lengths = lengths.at[donor].add(-moved).at[receiver].add(moved)
    items = jnp.searchsorted(jnp.cumsum(lengths), jnp.arange(rows * top), side="right").astype(jnp.int32)
    table = items.reshape(top, rows).T
    table = table[jax.random.permutation(jax.random.fold_in(own, 1), rows)]
    rotation = jax.random.randint(jax.random.fold_in(own, 2), (rows, 1), 0, top)
    return jnp.take_along_axis(table, (jnp.arange(top)[None, :] + rotation) % top, axis=1)


def portions_of(number_of, total, most, skew, full):
    portions = [(1 << 20) // math.isqrt(standing ** skew) + 1 for standing in range(1, number_of + 1)]
    largest = most if full else min(most, max(-(-total // number_of), total * portions[0] // sum(portions)))
    least = 1 if total - largest >= number_of - 1 else 0
    holding, spare = [largest] + [least] * (number_of - 1), total - largest - least * (number_of - 1)
    while spare > 0:
        movable = [i for i in range(1, number_of) if holding[i] < largest] or [i for i in range(1, number_of) if holding[i] < most]
        pool, left = sum([portions[i] for i in movable]), spare
        for i in movable:
            extra = min(most - holding[i], max(1, left * portions[i] // pool), spare)
            holding[i] = holding[i] + extra
            spare = spare - extra
    return np.array(holding)


def centred(stream_key, dims, scale, reach, pieces=(), kind=jnp.bfloat16):
    array = scale * jax.random.normal(stream_key, dims, jnp.float32)
    if pieces:
        array = array * block_scale(stream_key, dims, pieces, -0.22, 0.18)
    return jnp.clip(array, -reach, reach).astype(kind)


def setup_inputs(seed: int = 0) -> dict:
    arg_keys = jax.random.split(jax.random.key(seed), 10)
    queries = draw_queries(jax.random.fold_in(arg_keys[9], 71), 0)
    keys = draw_keys(jax.random.fold_in(arg_keys[9], 71), 0)
    values = centred(arg_keys[2], (TOKENS, KV_HEADS * HEAD_DIM), 1.0, 6.0, ((0, 32),))
    norm_gain = jnp.clip(1.0 + 0.18 * jax.random.normal(arg_keys[3], (D,), jnp.float32), 0.1, 1.9)
    expert_ids_keys = jax.random.split(jax.random.fold_in(arg_keys[4], 1), TOKENS // TOK_DEV)
    expert_ids_turns = jax.random.permutation(jax.random.fold_in(arg_keys[4], 3), TOKENS // TOK_DEV)
    expert_ids = jax.vmap(lambda own, number: routed_block(jax.random.fold_in(arg_keys[4], 2), own, number, TOK_DEV, EXPERTS, TOP, CAP, 1))(expert_ids_keys, expert_ids_turns).reshape((TOKENS, TOP))
    gate_values = jnp.clip(jnp.exp(math.log(1.0) - 2.3025851 * jax.random.uniform(arg_keys[5], (TOKENS, TOP), jnp.float32) ** block_scale(arg_keys[5], (TOKENS, TOP), ((0, 32),), -0.2, 0.2)), 0.1, 1.0)
    hidden_grad = centred(arg_keys[6], (TOKENS, FF), 0.1, 0.59765625, ((0, 32),))
    gate_weight = centred(arg_keys[7], (EXPERTS, D, FF), D ** -0.5, 0.125, ((0, 4), (2, 2)))
    up_weight = centred(arg_keys[8], (EXPERTS, D, FF), D ** -0.5, 0.125, ((0, 4), (2, 2)))
    return {"queries": queries, "keys": keys, "values": values, "norm_gain": norm_gain, "expert_ids": expert_ids, "gate_values": gate_values, "hidden_grad": hidden_grad, "gate_weight": gate_weight, "up_weight": up_weight}


epsilon = 1e-05
masked_score = -1e+30

def attend_sequence(operands, norm_gain):
    query_rows, key_rows, value_rows = operands
    length_here = query_rows.shape[0]
    group_size = HEADS // KV_HEADS
    query_heads = query_rows.reshape(length_here, KV_HEADS, group_size, HEAD_DIM).astype(jnp.float32)
    key_heads = key_rows.reshape(length_here, KV_HEADS, HEAD_DIM).astype(jnp.float32)
    value_heads = value_rows.reshape(length_here, KV_HEADS, HEAD_DIM).astype(jnp.float32)
    scores = jnp.einsum('tkgd,rkd->tkgr', query_heads, key_heads) * (1.0 / math.sqrt(HEAD_DIM))
    positions = jnp.arange(length_here, dtype=jnp.int32)
    allowed = (positions[None, :] <= positions[:, None])[:, None, None, :]
    scores = jnp.where(allowed, scores, masked_score)
    row_max = lax.optimization_barrier(jnp.max(scores, axis=-1, keepdims=True))
    exponent_terms = jnp.where(allowed, jnp.exp(scores - row_max), 0.0)
    denominator = lax.optimization_barrier(jnp.sum(exponent_terms, axis=-1))
    rounded = lax.optimization_barrier(exponent_terms.astype(jnp.bfloat16)).astype(jnp.float32)
    attended = jnp.einsum('tkgr,rkd->tkgd', rounded, value_heads) / denominator[..., None]
    attended = attended.reshape(length_here, HEADS * HEAD_DIM)
    mean_square = lax.optimization_barrier(jnp.mean(attended * attended, axis=-1, keepdims=True))
    return (attended * lax.rsqrt(mean_square + epsilon) * norm_gain).astype(jnp.bfloat16)

def replica_gradient(operands, gate_weight, up_weight):
    normed_rows, id_rows, gate_rows, grad_rows = operands
    flat_ids = id_rows.reshape(-1)
    flat_gates = gate_rows.reshape(-1)
    most_rows = N_EP * N_SQ * CAP

    def one_expert(expert_operands):
        expert_index, weight_gate, weight_up = expert_operands
        hit = flat_ids == expert_index
        order = jnp.argsort(jnp.where(hit, 0, 1).astype(jnp.int32), stable=True)[:most_rows].astype(jnp.int32)
        valid = hit[order]
        token_index = order // TOP
        inputs = jnp.where(valid[:, None], normed_rows[token_index], jnp.zeros((), jnp.bfloat16))
        scaled = flat_gates[order][:, None] * grad_rows[token_index].astype(jnp.float32)
        cotangent = jnp.where(valid[:, None], scaled, 0.0).astype(jnp.bfloat16)
        pre_gate = jnp.dot(inputs, weight_gate, preferred_element_type=jnp.float32)
        pre_up = jnp.dot(inputs, weight_up, preferred_element_type=jnp.float32)
        sigmoid_gate = jax.nn.sigmoid(pre_gate)
        slope = sigmoid_gate * (1.0 + pre_gate * (1.0 - sigmoid_gate))
        delta_gate = (cotangent.astype(jnp.float32) * pre_up * slope).astype(jnp.bfloat16)
        return jnp.dot(inputs.T, delta_gate, preferred_element_type=jnp.float32)
    expert_range = jnp.arange(EXPERTS, dtype=jnp.int32)
    return lax.map(one_expert, (expert_range, gate_weight, up_weight))

def reference(queries, keys, values, norm_gain, expert_ids, gate_values, hidden_grad, gate_weight, up_weight):
    sequences = TOKENS // LENGTH

    def attend_one(operands):
        return attend_sequence(operands, norm_gain)
    normed = lax.map(attend_one, (queries.reshape(sequences, LENGTH, D), keys.reshape(sequences, LENGTH, KV_HEADS * HEAD_DIM), values.reshape(sequences, LENGTH, KV_HEADS * HEAD_DIM)))
    normed = normed.reshape(REPLICAS, REPLICA_TOKENS, D)
    id_blocks = expert_ids.reshape(REPLICAS, REPLICA_TOKENS, TOP)
    gate_blocks = gate_values.reshape(REPLICAS, REPLICA_TOKENS, TOP)
    grad_blocks = hidden_grad.reshape(REPLICAS, REPLICA_TOKENS, FF)

    def add_replica(accumulated, operands):
        replica_part = replica_gradient(operands, gate_weight, up_weight)
        rounded = lax.optimization_barrier(replica_part.astype(jnp.bfloat16))
        return (accumulated + rounded.astype(jnp.float32), None)
    initial = jnp.zeros((EXPERTS, D, FF), jnp.float32)
    result, unused = lax.scan(add_replica, initial, (normed, id_blocks, gate_blocks, grad_blocks))
    return result
```

```python
import functools
import math

import jax
import jax.numpy as jnp
from jax import lax
from jax.experimental import pallas as pl
from jax.experimental.pallas import tpu as pltpu
from jax.sharding import PartitionSpec as P

HEAD_DIM = 128

epsilon = 1e-05
masked_score = -1e30


def attention_kernel(group_size, shard_ref, q_ref, ko_ref, vo_ref, kp_ref, vp_ref, gain_ref, out_ref, acc_ref):
    rows, model_width = q_ref.shape
    past = kp_ref.shape[0]
    scale = 1.0 / math.sqrt(HEAD_DIM)
    shard = shard_ref[0]
    contract = (((1,), (1,)), ((), ()))
    causal = lax.broadcasted_iota(jnp.int32, (rows, rows), 1) <= lax.broadcasted_iota(
        jnp.int32, (rows, rows), 0
    )
    seen = lax.broadcasted_iota(jnp.int32, (rows, past), 1) < shard * rows
    squares = jnp.zeros((rows, 1), jnp.float32)
    for head in range(model_width // HEAD_DIM):
        cols = slice(head * HEAD_DIM, (head + 1) * HEAD_DIM)
        kv = head // group_size
        kv_cols = slice(kv * HEAD_DIM, (kv + 1) * HEAD_DIM)
        q = q_ref[:, cols]
        own = lax.dot_general(q, ko_ref[:, kv_cols], contract, preferred_element_type=jnp.float32)
        old = lax.dot_general(q, kp_ref[:, kv_cols], contract, preferred_element_type=jnp.float32)
        own = jnp.where(causal, own * scale, masked_score)
        old = jnp.where(seen, old * scale, masked_score)
        top = jnp.maximum(
            jnp.max(own, axis=1, keepdims=True), jnp.max(old, axis=1, keepdims=True)
        )
        own = jnp.exp(own - top)
        old = jnp.exp(old - top)
        total = jnp.sum(own, axis=1, keepdims=True) + jnp.sum(old, axis=1, keepdims=True)
        out = jnp.dot(
            own.astype(jnp.bfloat16), vo_ref[:, kv_cols], preferred_element_type=jnp.float32
        ) + jnp.dot(
            old.astype(jnp.bfloat16), vp_ref[:, kv_cols], preferred_element_type=jnp.float32
        )
        out = out / total
        acc_ref[:, cols] = out
        squares = squares + jnp.sum(out * out, axis=1, keepdims=True)
    inverse = lax.rsqrt(squares / model_width + epsilon)
    out_ref[...] = (acc_ref[...] * inverse * gain_ref[...]).astype(jnp.bfloat16)


def attend(shard, queries, keys, values, past_keys, past_values, norm_gain):
    rows, model_width = queries.shape
    group_size = model_width // keys.shape[1]
    vmem = pl.BlockSpec(memory_space=pltpu.VMEM)
    return pl.pallas_call(
        functools.partial(attention_kernel, group_size),
        out_shape=jax.ShapeDtypeStruct((rows, model_width), jnp.bfloat16),
        in_specs=[pl.BlockSpec(memory_space=pltpu.SMEM)] + [vmem] * 6,
        out_specs=vmem,
        scratch_shapes=[pltpu.VMEM((rows, model_width), jnp.float32)],
        compiler_params=pltpu.CompilerParams(vmem_limit_bytes=32 << 20),
        cost_estimate=pl.CostEstimate(
            flops=4 * rows * model_width * (rows + past_keys.shape[0]),
            bytes_accessed=4 * rows * model_width,
            transcendentals=rows * (model_width // HEAD_DIM) * (rows + past_keys.shape[0]),
        ),
    )(shard.reshape(1), queries, keys, values, past_keys, past_values, norm_gain.reshape(1, -1))


def ring(size, shift):
    return [(i, (i + shift) % size) for i in range(size)]


def body(
    queries, keys, values, norm_gain, expert_ids, gate_values, hidden_grad, gate_weight, up_weight
):
    rows, model_width = queries.shape
    n_ep = lax.axis_size("ep")
    n_sq = lax.axis_size("sq")
    shard = lax.axis_index("sq")
    expert = lax.axis_index("ep")
    weight_gate = gate_weight[0]
    weight_up = up_weight[0]
    width = weight_gate.shape[1]
    kv_width = keys.shape[1]

    both = jnp.concatenate([keys, values], axis=1)
    past = []
    for j in range(1, n_sq):
        past.append(lax.ppermute(both, "sq", [(i, i + j) for i in range(n_sq - j)]))
    past = jnp.concatenate(past, axis=0)

    def columns_of(owner):
        return lax.dynamic_slice_in_dim(hidden_grad, owner * width, width, 1)

    grads = [columns_of(shard)]
    for j in range(1, n_sq):
        grads.append(lax.ppermute(columns_of((shard + j) % n_sq), "sq", ring(n_sq, j)))
    grad = jnp.concatenate(grads, axis=0)

    chosen = expert_ids[:, :, None] == jnp.arange(n_ep, dtype=jnp.int32)
    share = jnp.sum(jnp.where(chosen, gate_values[:, :, None], 0.0), axis=1).T
    shares = lax.all_gather(share, ("ep", "sq"), axis=0, tiled=False)
    shares = lax.dynamic_index_in_dim(shares, expert, 1, keepdims=False).reshape(n_ep, n_sq, rows)
    order = (shard - jnp.arange(n_sq)) % n_sq
    shares = jnp.take(shares, order, axis=1).reshape(n_ep, n_sq * rows)

    normed = attend(
        shard, queries, keys, values, past[:, :kv_width], past[:, kv_width:], norm_gain
    )

    def add_chunk(step, tokens, grad, summed):
        source = (expert - step) % n_ep
        share_here = lax.dynamic_index_in_dim(shares, source, 0, keepdims=False)
        pieces = [tokens]
        for j in range(1, n_sq):
            pieces.append(lax.ppermute(tokens, "sq", ring(n_sq, j)))
        for j, inputs in enumerate(pieces):
            part = slice(j * rows, (j + 1) * rows)
            cotangent = (share_here[part, None] * grad[part].astype(jnp.float32)).astype(
                jnp.bfloat16
            )
            pre_gate = jnp.dot(inputs, weight_gate, preferred_element_type=jnp.float32)
            pre_up = jnp.dot(inputs, weight_up, preferred_element_type=jnp.float32)
            sigmoid_gate = jax.nn.sigmoid(pre_gate)
            slope = sigmoid_gate * (1.0 + pre_gate * (1.0 - sigmoid_gate))
            delta = (cotangent.astype(jnp.float32) * pre_up * slope).astype(jnp.bfloat16)
            term = lax.dot_general(
                inputs, delta, (((0,), (0,)), ((), ())), preferred_element_type=jnp.float32
            )
            summed = term if summed is None else summed + term
        return summed

    def turn(tokens, grad):
        return lax.ppermute(tokens, "ep", ring(n_ep, 1)), lax.ppermute(grad, "ep", ring(n_ep, 1))

    if n_ep <= 8:
        summed = None
        tokens = normed
        for step in range(n_ep):
            if step < n_ep - 1:
                turned = turn(tokens, grad)
            summed = add_chunk(step, tokens, grad, summed)
            if step < n_ep - 1:
                tokens, grad = turned
    else:

        def one_step(step, carried):
            tokens, grad, summed = carried
            turned = turn(tokens, grad)
            return (*turned, add_chunk(step, tokens, grad, summed))

        start = jnp.zeros((model_width, width), jnp.float32)
        summed = lax.fori_loop(0, n_ep, one_step, (normed, grad, start))[2]
    return lax.psum_scatter(
        summed[None].astype(jnp.bfloat16), "grp", scatter_dimension=1, tiled=True
    ).astype(jnp.float32)


def solution(mesh):
    return jax.shard_map(
        body,
        mesh=mesh,
        in_specs=(
            P(("grp", "ep", "sq"), None),
            P(("grp", "ep", "sq"), None),
            P(("grp", "ep", "sq"), None),
            P(),
            P(("grp", "ep", "sq"), None),
            P(("grp", "ep", "sq"), None),
            P(("grp", "ep", "sq"), None),
            P("ep", None, "sq"),
            P("ep", None, "sq"),
        ),
        out_specs=P("ep", "grp", "sq"),
        check_vma=False,
    )
```

```python
import functools
import math

import jax
import jax.numpy as jnp
from jax import lax
from jax.experimental import pallas as pl
from jax.experimental.pallas import tpu as pltpu
from jax.sharding import PartitionSpec as P

HEAD_DIM = 128

epsilon = 1e-05
masked_score = -1e30
MESH = pl.DeviceIdType.MESH


def attention_kernel(group_size, shard_ref, q_ref, ko_ref, vo_ref, kp_ref, vp_ref, gain_ref, out_ref, acc_ref):
    rows, model_width = q_ref.shape
    past = kp_ref.shape[0]
    scale = 1.0 / math.sqrt(HEAD_DIM)
    shard = shard_ref[0]
    contract = (((1,), (1,)), ((), ()))
    causal = lax.broadcasted_iota(jnp.int32, (rows, rows), 1) <= lax.broadcasted_iota(
        jnp.int32, (rows, rows), 0
    )
    seen = lax.broadcasted_iota(jnp.int32, (rows, past), 1) < shard * rows
    squares = jnp.zeros((rows, 1), jnp.float32)
    for head in range(model_width // HEAD_DIM):
        cols = slice(head * HEAD_DIM, (head + 1) * HEAD_DIM)
        kv = head // group_size
        kv_cols = slice(kv * HEAD_DIM, (kv + 1) * HEAD_DIM)
        q = q_ref[:, cols]
        own = lax.dot_general(q, ko_ref[:, kv_cols], contract, preferred_element_type=jnp.float32)
        old = lax.dot_general(q, kp_ref[:, kv_cols], contract, preferred_element_type=jnp.float32)
        own = jnp.where(causal, own * scale, masked_score)
        old = jnp.where(seen, old * scale, masked_score)
        top = jnp.maximum(
            jnp.max(own, axis=1, keepdims=True), jnp.max(old, axis=1, keepdims=True)
        )
        own = jnp.exp(own - top)
        old = jnp.exp(old - top)
        total = jnp.sum(own, axis=1, keepdims=True) + jnp.sum(old, axis=1, keepdims=True)
        out = jnp.dot(
            own.astype(jnp.bfloat16), vo_ref[:, kv_cols], preferred_element_type=jnp.float32
        ) + jnp.dot(
            old.astype(jnp.bfloat16), vp_ref[:, kv_cols], preferred_element_type=jnp.float32
        )
        out = out / total
        acc_ref[:, cols] = out
        squares = squares + jnp.sum(out * out, axis=1, keepdims=True)
    inverse = lax.rsqrt(squares / model_width + epsilon)
    out_ref[...] = (acc_ref[...] * inverse * gain_ref[...]).astype(jnp.bfloat16)


def attend(shard, queries, keys, values, past_keys, past_values, norm_gain):
    rows, model_width = queries.shape
    group_size = model_width // keys.shape[1]
    vmem = pl.BlockSpec(memory_space=pltpu.VMEM)
    return pl.pallas_call(
        functools.partial(attention_kernel, group_size),
        out_shape=jax.ShapeDtypeStruct((rows, model_width), jnp.bfloat16),
        in_specs=[pl.BlockSpec(memory_space=pltpu.SMEM)] + [vmem] * 6,
        out_specs=vmem,
        scratch_shapes=[pltpu.VMEM((rows, model_width), jnp.float32)],
        compiler_params=pltpu.CompilerParams(vmem_limit_bytes=32 << 20),
        cost_estimate=pl.CostEstimate(
            flops=4 * rows * model_width * (rows + past_keys.shape[0]),
            bytes_accessed=4 * rows * model_width,
            transcendentals=rows * (model_width // HEAD_DIM) * (rows + past_keys.shape[0]),
        ),
    )(shard.reshape(1), queries, keys, values, past_keys, past_values, norm_gain.reshape(1, -1))


def ring(size, shift):
    return [(i, (i + shift) % size) for i in range(size)]


def body(
    queries, keys, values, norm_gain, expert_ids, gate_values, hidden_grad, gate_weight, up_weight
):
    rows, model_width = queries.shape
    n_ep = lax.axis_size("ep")
    n_sq = lax.axis_size("sq")
    shard = lax.axis_index("sq")
    expert = lax.axis_index("ep")
    weight_gate = gate_weight[0]
    weight_up = up_weight[0]
    width = weight_gate.shape[1]
    kv_width = keys.shape[1]

    both = jnp.concatenate([keys, values], axis=1)
    past = []
    for j in range(1, n_sq):
        past.append(lax.ppermute(both, "sq", [(i, i + j) for i in range(n_sq - j)]))
    past = jnp.concatenate(past, axis=0)

    def columns_of(owner):
        return lax.dynamic_slice_in_dim(hidden_grad, owner * width, width, 1)

    grads = [columns_of(shard)]
    for j in range(1, n_sq):
        grads.append(lax.ppermute(columns_of((shard + j) % n_sq), "sq", ring(n_sq, j)))
    grad = jnp.concatenate(grads, axis=0)

    chosen = expert_ids[:, :, None] == jnp.arange(n_ep, dtype=jnp.int32)
    share = jnp.sum(jnp.where(chosen, gate_values[:, :, None], 0.0), axis=1).T
    shares = lax.all_gather(share, ("ep", "sq"), axis=0, tiled=False)
    shares = lax.dynamic_index_in_dim(shares, expert, 1, keepdims=False).reshape(n_ep, n_sq, rows)
    order = (shard - jnp.arange(n_sq)) % n_sq
    shares = jnp.take(shares, order, axis=1).reshape(n_ep, n_sq * rows)

    normed = attend(
        shard, queries, keys, values, past[:, :kv_width], past[:, kv_width:], norm_gain
    )

    def add_chunk(step, tokens, grad, summed):
        source = (expert - step) % n_ep
        share_here = lax.dynamic_index_in_dim(shares, source, 0, keepdims=False)
        pieces = [tokens]
        for j in range(1, n_sq):
            pieces.append(lax.ppermute(tokens, "sq", ring(n_sq, j)))
        for j, inputs in enumerate(pieces):
            part = slice(j * rows, (j + 1) * rows)
            cotangent = (share_here[part, None] * grad[part].astype(jnp.float32)).astype(
                jnp.bfloat16
            )
            pre_gate = jnp.dot(inputs, weight_gate, preferred_element_type=jnp.float32)
            pre_up = jnp.dot(inputs, weight_up, preferred_element_type=jnp.float32)
            sigmoid_gate = jax.nn.sigmoid(pre_gate)
            slope = sigmoid_gate * (1.0 + pre_gate * (1.0 - sigmoid_gate))
            delta = (cotangent.astype(jnp.float32) * pre_up * slope).astype(jnp.bfloat16)
            term = lax.dot_general(
                inputs, delta, (((0,), (0,)), ((), ())), preferred_element_type=jnp.float32
            )
            summed = term if summed is None else summed + term
        return summed

    def turn(tokens, grad):
        return lax.ppermute(tokens, "ep", ring(n_ep, 1)), lax.ppermute(grad, "ep", ring(n_ep, 1))

    if n_ep <= 8:
        summed = None
        tokens = normed
        for step in range(n_ep):
            if step < n_ep - 1:
                turned = turn(tokens, grad)
            summed = add_chunk(step, tokens, grad, summed)
            if step < n_ep - 1:
                tokens, grad = turned
    else:

        def one_step(step, carried):
            tokens, grad, summed = carried
            turned = turn(tokens, grad)
            return (*turned, add_chunk(step, tokens, grad, summed))

        start = jnp.zeros((model_width, width), jnp.float32)
        summed = lax.fori_loop(0, n_ep, one_step, (normed, grad, start))[2]
    return lax.psum_scatter(
        summed[None].astype(jnp.bfloat16), "grp", scatter_dimension=1, tiled=True
    ).astype(jnp.float32)


def whole_kernel(
    q_ref, k_ref, v_ref, gain_ref, share_ref, hidden_ref, gate_hbm, up_hbm, out_ref,
    x_buf, g_buf, c_buf, kv_buf, weight_gate, weight_up, delta_ref, attended, acc,
    stage, from_core, carry, from_chip,
    load_sem, kv_send, kv_recv, yg_send, yg_recv, zg_send, zg_recv, zc_send, zc_recv,
    zx_send, zx_recv, yx_send, yx_recv, core_send, core_recv, chip_send, chip_recv,
):
    n_ep = x_buf.shape[0]
    rows, model_width = q_ref.shape
    width = weight_gate.shape[1]
    kv_heads = k_ref.shape[1] // HEAD_DIM
    group_size = model_width // k_ref.shape[1]
    half = rows // 2
    block = model_width // 4
    scale = 1.0 / math.sqrt(HEAD_DIM)
    grp, expert, shard = lax.axis_index("grp"), lax.axis_index("ep"), lax.axis_index("sq")
    peer = 1 - shard
    right, left = lax.rem(expert + 1, n_ep), lax.rem(expert + n_ep - 1, n_ep)
    core = lax.rem(grp, 2)
    chip = grp // 2
    sibling = chip * 2 + 1 - core
    across = (1 - chip) * 2 + core
    diagonal = (1 - chip) * 2 + 1 - core

    loads = [
        pltpu.make_async_copy(gate_hbm, weight_gate, load_sem.at[0]),
        pltpu.make_async_copy(up_hbm, weight_up, load_sem.at[1]),
    ]
    for load in loads:
        load.start()

    barrier = pltpu.get_barrier_semaphore()
    for target in ({"sq": peer}, {"ep": right}, {"ep": left}, {"grp": sibling}, {"grp": across}):
        pl.semaphore_signal(barrier, inc=1, device_id=target, device_id_type=MESH)
    pl.semaphore_wait(barrier, 5)

    def send(src, dst, send_sem, recv_sem, target):
        return pltpu.make_async_remote_copy(
            src_ref=src, dst_ref=dst, send_sem=send_sem, recv_sem=recv_sem,
            device_id=target, device_id_type=MESH,
        )

    def part(h):
        return pl.ds(pl.multiple_of(h * half, half), half)

    def zx(s, h):
        return send(x_buf.at[s, 0, part(h)], x_buf.at[s + 1, 0, part(h)],
                    zx_send.at[s, h], zx_recv.at[s, h], {"ep": right})

    def yx(s, h):
        return send(x_buf.at[s, 0, part(h)], x_buf.at[s, 1, part(h)],
                    yx_send.at[s, h], yx_recv.at[s, h], {"sq": peer})

    def zg(s, j):
        return send(g_buf.at[s, j], g_buf.at[s + 1, j],
                    zg_send.at[s, j], zg_recv.at[s, j], {"ep": right})

    def zc(s, j):
        return send(c_buf.at[s, j], c_buf.at[s + 1, j],
                    zc_send.at[s, j], zc_recv.at[s, j], {"ep": right})

    y_keys = send(k_ref, kv_buf.at[0], kv_send.at[0], kv_recv.at[0], {"sq": peer})
    y_values = send(v_ref, kv_buf.at[1], kv_send.at[1], kv_recv.at[1], {"sq": peer})
    peer_columns = pl.ds(pl.multiple_of(peer * width, width), width)
    own_columns = pl.ds(pl.multiple_of(shard * width, width), width)
    y_grad = send(hidden_ref.at[:, peer_columns], g_buf.at[0, 1],
                  yg_send.at[0], yg_recv.at[0], {"sq": peer})
    y_share = send(share_ref, c_buf.at[0, 1], yg_send.at[1], yg_recv.at[1], {"sq": peer})
    y_keys.start()
    y_values.start()
    y_share.start()
    y_grad.start()
    g_buf[0, 0] = hidden_ref[:, own_columns]
    c_buf[0, 0] = share_ref[...]
    zc(0, 0).start()
    zg(0, 0).start()
    acc[...] = jnp.zeros_like(acc)
    y_keys.wait_recv()
    y_values.wait_recv()

    contract = (((1,), (1,)), ((), ()))

    @pl.loop(0, 2)
    def _(h):
        causal = lax.broadcasted_iota(jnp.int32, (half, rows), 1) <= (
            lax.broadcasted_iota(jnp.int32, (half, rows), 0) + h * half
        )
        seen = lax.broadcasted_iota(jnp.int32, (half, rows), 1) < shard * rows
        squares = jnp.zeros((half, 1), jnp.float32)
        for head in range(kv_heads * group_size):
            cols = slice(head * HEAD_DIM, (head + 1) * HEAD_DIM)
            kv = head // group_size
            kv_cols = slice(kv * HEAD_DIM, (kv + 1) * HEAD_DIM)
            q = q_ref[part(h), cols]
            own = lax.dot_general(
                q, k_ref[:, kv_cols], contract, preferred_element_type=jnp.float32
            )
            old = lax.dot_general(
                q, kv_buf[0, :, kv_cols], contract, preferred_element_type=jnp.float32
            )
            own = jnp.where(causal, own * scale, masked_score)
            old = jnp.where(seen, old * scale, masked_score)
            top = jnp.maximum(
                jnp.max(own, axis=1, keepdims=True), jnp.max(old, axis=1, keepdims=True)
            )
            own = jnp.exp(own - top)
            old = jnp.exp(old - top)
            total = jnp.sum(own, axis=1, keepdims=True) + jnp.sum(old, axis=1, keepdims=True)
            out = jnp.dot(
                own.astype(jnp.bfloat16), v_ref[:, kv_cols], preferred_element_type=jnp.float32
            ) + jnp.dot(
                old.astype(jnp.bfloat16), kv_buf[1, :, kv_cols],
                preferred_element_type=jnp.float32,
            )
            out = out / total
            attended[:, cols] = out
            squares = squares + jnp.sum(out * out, axis=1, keepdims=True)
        inverse = lax.rsqrt(squares / model_width + epsilon)
        x_buf[0, 0, part(h)] = (attended[...] * inverse * gain_ref[...]).astype(jnp.bfloat16)
        zx(0, h).start()
        yx(0, h).start()

    y_share.wait_recv()
    y_grad.wait_recv()
    zc(0, 1).start()
    zg(0, 1).start()
    for load in loads:
        load.wait()

    tile = min(256, width)

    def deltas(s, j):
        share = c_buf[s, j]
        picked = lax.broadcasted_iota(jnp.int32, share.shape, 0) == expert
        share = jnp.sum(jnp.where(picked, share, 0.0), axis=0, keepdims=True)
        share = jnp.broadcast_to(share, (128, rows)).T[:, :1]

        @pl.loop(0, width // tile)
        def _(t):
            cols = pl.ds(pl.multiple_of(t * tile, tile), tile)
            inputs = x_buf[s, j]
            pre_gate = jnp.dot(inputs, weight_gate[:, cols], preferred_element_type=jnp.float32)
            pre_up = jnp.dot(inputs, weight_up[:, cols], preferred_element_type=jnp.float32)
            cotangent = (share * g_buf[s, j, :, cols].astype(jnp.float32)).astype(jnp.bfloat16)
            sigmoid_gate = 1.0 / (1.0 + jnp.exp(-pre_gate))
            slope = sigmoid_gate * (1.0 + pre_gate * (1.0 - sigmoid_gate))
            delta_ref[:, cols] = (cotangent.astype(jnp.float32) * pre_up * slope).astype(
                jnp.bfloat16
            )

    def columns(b):
        return pl.ds(pl.multiple_of(b * block, block), block)

    def add_block(s, j, b):
        return acc[:, columns(b)] + lax.dot_general(
            delta_ref[...], x_buf[s, j, :, columns(b)], (((0,), (0,)), ((), ())),
            preferred_element_type=jnp.float32,
        )

    def add_piece(s, j):
        deltas(s, j)

        @pl.loop(0, 4)
        def _(b):
            acc[:, columns(b)] = add_block(s, j, b)

    @pl.loop(1, n_ep)
    def _(s):
        for j in range(2):
            zc(s - 1, j).wait_recv()
            zg(s - 1, j).wait_recv()

            @pl.when(s < n_ep - 1)
            def _():
                zc(s, j).start()
                zg(s, j).start()

            zx(s - 1, j).wait_recv()

            @pl.when(s < n_ep - 1)
            def _():
                zx(s, j).start()

            yx(s, j).start()
            if j == 1:
                yx(s - 1, 0).wait_recv()
                yx(s - 1, 1).wait_recv()
            add_piece(s - 1, j)

    last = n_ep - 1
    add_piece(last, 0)
    yx(last, 0).wait_recv()
    yx(last, 1).wait_recv()
    deltas(last, 1)

    def to_core(i):
        return send(stage.at[i], from_core.at[i], core_send.at[i], core_recv.at[i],
                    {"grp": sibling})

    to_chip = send(carry, from_chip, chip_send, chip_recv, {"grp": across})
    stage[0] = add_block(last, 1, diagonal).astype(jnp.bfloat16)
    to_core(0).start()
    mine = add_block(last, 1, across)
    to_core(0).wait_recv()
    carry[...] = (mine + from_core[0].astype(jnp.float32)).astype(jnp.bfloat16)
    to_chip.start()
    stage[1] = add_block(last, 1, sibling).astype(jnp.bfloat16)
    to_core(1).start()
    acc[:, columns(grp)] = add_block(last, 1, grp)
    to_core(1).wait_recv()
    acc[:, columns(grp)] += from_core[1].astype(jnp.float32)
    to_chip.wait_recv()
    out_ref[...] = (acc[:, columns(grp)] + from_chip[...].astype(jnp.float32)).T

    for copy in (y_keys, y_values, y_share, y_grad, to_core(0), to_core(1), to_chip):
        copy.wait_send()

    @pl.loop(0, n_ep)
    def _(s):
        for j in range(2):
            yx(s, j).wait_send()

            @pl.when(s < n_ep - 1)
            def _():
                zx(s, j).wait_send()
                zg(s, j).wait_send()
                zc(s, j).wait_send()


def fused(
    queries, keys, values, norm_gain, expert_ids, gate_values, hidden_grad, gate_weight, up_weight
):
    rows, model_width = queries.shape
    n_ep = lax.axis_size("ep")
    width = gate_weight.shape[2]
    kv_width = keys.shape[1]
    block = model_width // 4
    chosen = expert_ids.T[:, None, :] == jnp.arange(8, dtype=jnp.int32)[:, None]
    share = jnp.sum(jnp.where(chosen, gate_values.T[:, None, :], 0.0), axis=0)
    vmem = pl.BlockSpec(memory_space=pltpu.VMEM)
    hbm = pl.BlockSpec(memory_space=pl.ANY)
    dma = pltpu.SemaphoreType.DMA
    bf16, f32 = jnp.bfloat16, jnp.float32
    out = pl.pallas_call(
        whole_kernel,
        out_shape=jax.ShapeDtypeStruct((block, width), f32),
        in_specs=[vmem] * 6 + [hbm] * 2,
        out_specs=vmem,
        scratch_shapes=[
            pltpu.VMEM((n_ep, 2, rows, model_width), bf16),
            pltpu.VMEM((n_ep, 2, rows, width), bf16),
            pltpu.VMEM((n_ep, 2, 8, rows), f32),
            pltpu.VMEM((2, rows, kv_width), bf16),
            pltpu.VMEM((model_width, width), bf16),
            pltpu.VMEM((model_width, width), bf16),
            pltpu.VMEM((rows, width), bf16),
            pltpu.VMEM((rows // 2, model_width), f32),
            pltpu.VMEM((width, model_width), f32),
            pltpu.VMEM((2, width, block), bf16),
            pltpu.VMEM((2, width, block), bf16),
            pltpu.VMEM((width, block), bf16),
            pltpu.VMEM((width, block), bf16),
            dma((2,)), dma((2,)), dma((2,)), dma((2,)), dma((2,)),
            dma((n_ep, 2)), dma((n_ep, 2)), dma((n_ep, 2)), dma((n_ep, 2)),
            dma((n_ep, 2)), dma((n_ep, 2)), dma((n_ep, 2)), dma((n_ep, 2)),
            dma((2,)), dma((2,)), dma, dma,
        ],
        compiler_params=pltpu.CompilerParams(
            collective_id=0, has_side_effects=True, vmem_limit_bytes=48 << 20
        ),
    )(
        queries, keys, values, norm_gain.reshape(1, -1), share, hidden_grad,
        gate_weight[0], up_weight[0],
    )
    return out[None]


def solution(mesh):
    small = mesh.shape["grp"] == 4 and mesh.shape["sq"] == 2 and 3 <= mesh.shape["ep"] <= 8
    return jax.shard_map(
        fused if small else body,
        mesh=mesh,
        in_specs=(
            P(("grp", "ep", "sq"), None),
            P(("grp", "ep", "sq"), None),
            P(("grp", "ep", "sq"), None),
            P(),
            P(("grp", "ep", "sq"), None),
            P(("grp", "ep", "sq"), None),
            P(("grp", "ep", "sq"), None),
            P("ep", None, "sq"),
            P("ep", None, "sq"),
        ),
        out_specs=P("ep", "grp", "sq"),
        check_vma=False,
    )
```

```python
import functools
import math

import jax
import jax.numpy as jnp
from jax import lax
from jax.experimental import pallas as pl
from jax.experimental.pallas import tpu as pltpu
from jax.sharding import PartitionSpec as P

HEAD_DIM = 128

epsilon = 1e-05
masked_score = -1e30
MESH = pl.DeviceIdType.MESH


def attention_kernel(group_size, shard_ref, q_ref, ko_ref, vo_ref, kp_ref, vp_ref, gain_ref, out_ref, acc_ref):
    rows, model_width = q_ref.shape
    past = kp_ref.shape[0]
    scale = 1.0 / math.sqrt(HEAD_DIM)
    shard = shard_ref[0]
    contract = (((1,), (1,)), ((), ()))
    causal = lax.broadcasted_iota(jnp.int32, (rows, rows), 1) <= lax.broadcasted_iota(
        jnp.int32, (rows, rows), 0
    )
    seen = lax.broadcasted_iota(jnp.int32, (rows, past), 1) < shard * rows
    squares = jnp.zeros((rows, 1), jnp.float32)
    for head in range(model_width // HEAD_DIM):
        cols = slice(head * HEAD_DIM, (head + 1) * HEAD_DIM)
        kv = head // group_size
        kv_cols = slice(kv * HEAD_DIM, (kv + 1) * HEAD_DIM)
        q = q_ref[:, cols]
        own = lax.dot_general(q, ko_ref[:, kv_cols], contract, preferred_element_type=jnp.float32)
        old = lax.dot_general(q, kp_ref[:, kv_cols], contract, preferred_element_type=jnp.float32)
        own = jnp.where(causal, own * scale, masked_score)
        old = jnp.where(seen, old * scale, masked_score)
        top = jnp.maximum(
            jnp.max(own, axis=1, keepdims=True), jnp.max(old, axis=1, keepdims=True)
        )
        own = jnp.exp(own - top)
        old = jnp.exp(old - top)
        total = jnp.sum(own, axis=1, keepdims=True) + jnp.sum(old, axis=1, keepdims=True)
        out = jnp.dot(
            own.astype(jnp.bfloat16), vo_ref[:, kv_cols], preferred_element_type=jnp.float32
        ) + jnp.dot(
            old.astype(jnp.bfloat16), vp_ref[:, kv_cols], preferred_element_type=jnp.float32
        )
        out = out / total
        acc_ref[:, cols] = out
        squares = squares + jnp.sum(out * out, axis=1, keepdims=True)
    inverse = lax.rsqrt(squares / model_width + epsilon)
    out_ref[...] = (acc_ref[...] * inverse * gain_ref[...]).astype(jnp.bfloat16)


def attend(shard, queries, keys, values, past_keys, past_values, norm_gain):
    rows, model_width = queries.shape
    group_size = model_width // keys.shape[1]
    vmem = pl.BlockSpec(memory_space=pltpu.VMEM)
    return pl.pallas_call(
        functools.partial(attention_kernel, group_size),
        out_shape=jax.ShapeDtypeStruct((rows, model_width), jnp.bfloat16),
        in_specs=[pl.BlockSpec(memory_space=pltpu.SMEM)] + [vmem] * 6,
        out_specs=vmem,
        scratch_shapes=[pltpu.VMEM((rows, model_width), jnp.float32)],
        compiler_params=pltpu.CompilerParams(vmem_limit_bytes=32 << 20),
        cost_estimate=pl.CostEstimate(
            flops=4 * rows * model_width * (rows + past_keys.shape[0]),
            bytes_accessed=4 * rows * model_width,
            transcendentals=rows * (model_width // HEAD_DIM) * (rows + past_keys.shape[0]),
        ),
    )(shard.reshape(1), queries, keys, values, past_keys, past_values, norm_gain.reshape(1, -1))


def ring(size, shift):
    return [(i, (i + shift) % size) for i in range(size)]


def body(
    queries, keys, values, norm_gain, expert_ids, gate_values, hidden_grad, gate_weight, up_weight
):
    rows, model_width = queries.shape
    n_ep = lax.axis_size("ep")
    n_sq = lax.axis_size("sq")
    shard = lax.axis_index("sq")
    expert = lax.axis_index("ep")
    weight_gate = gate_weight[0]
    weight_up = up_weight[0]
    width = weight_gate.shape[1]
    kv_width = keys.shape[1]

    both = jnp.concatenate([keys, values], axis=1)
    past = []
    for j in range(1, n_sq):
        past.append(lax.ppermute(both, "sq", [(i, i + j) for i in range(n_sq - j)]))
    past = jnp.concatenate(past, axis=0)

    def columns_of(owner):
        return lax.dynamic_slice_in_dim(hidden_grad, owner * width, width, 1)

    grads = [columns_of(shard)]
    for j in range(1, n_sq):
        grads.append(lax.ppermute(columns_of((shard + j) % n_sq), "sq", ring(n_sq, j)))
    grad = jnp.concatenate(grads, axis=0)

    chosen = expert_ids[:, :, None] == jnp.arange(n_ep, dtype=jnp.int32)
    share = jnp.sum(jnp.where(chosen, gate_values[:, :, None], 0.0), axis=1).T
    shares = lax.all_gather(share, ("ep", "sq"), axis=0, tiled=False)
    shares = lax.dynamic_index_in_dim(shares, expert, 1, keepdims=False).reshape(n_ep, n_sq, rows)
    order = (shard - jnp.arange(n_sq)) % n_sq
    shares = jnp.take(shares, order, axis=1).reshape(n_ep, n_sq * rows)

    normed = attend(
        shard, queries, keys, values, past[:, :kv_width], past[:, kv_width:], norm_gain
    )

    def add_chunk(step, tokens, grad, summed):
        source = (expert - step) % n_ep
        share_here = lax.dynamic_index_in_dim(shares, source, 0, keepdims=False)
        pieces = [tokens]
        for j in range(1, n_sq):
            pieces.append(lax.ppermute(tokens, "sq", ring(n_sq, j)))
        for j, inputs in enumerate(pieces):
            part = slice(j * rows, (j + 1) * rows)
            cotangent = (share_here[part, None] * grad[part].astype(jnp.float32)).astype(
                jnp.bfloat16
            )
            pre_gate = jnp.dot(inputs, weight_gate, preferred_element_type=jnp.float32)
            pre_up = jnp.dot(inputs, weight_up, preferred_element_type=jnp.float32)
            sigmoid_gate = jax.nn.sigmoid(pre_gate)
            slope = sigmoid_gate * (1.0 + pre_gate * (1.0 - sigmoid_gate))
            delta = (cotangent.astype(jnp.float32) * pre_up * slope).astype(jnp.bfloat16)
            term = lax.dot_general(
                inputs, delta, (((0,), (0,)), ((), ())), preferred_element_type=jnp.float32
            )
            summed = term if summed is None else summed + term
        return summed

    def turn(tokens, grad):
        return lax.ppermute(tokens, "ep", ring(n_ep, 1)), lax.ppermute(grad, "ep", ring(n_ep, 1))

    if n_ep <= 8:
        summed = None
        tokens = normed
        for step in range(n_ep):
            if step < n_ep - 1:
                turned = turn(tokens, grad)
            summed = add_chunk(step, tokens, grad, summed)
            if step < n_ep - 1:
                tokens, grad = turned
    else:

        def one_step(step, carried):
            tokens, grad, summed = carried
            turned = turn(tokens, grad)
            return (*turned, add_chunk(step, tokens, grad, summed))

        start = jnp.zeros((model_width, width), jnp.float32)
        summed = lax.fori_loop(0, n_ep, one_step, (normed, grad, start))[2]
    return lax.psum_scatter(
        summed[None].astype(jnp.bfloat16), "grp", scatter_dimension=1, tiled=True
    ).astype(jnp.float32)


def whole_kernel(
    q_hbm, k_hbm, v_hbm, gain_ref, share_ref, hidden_hbm, gate_hbm, up_hbm, out_ref,
    q_ref, k_ref, v_ref, x_full, x_comp, x_out, g_full, g_comp, g_out, c_buf, kv_buf,
    weight_gate, weight_up, delta_ref, attended, acc, stage, from_core, carry, from_chip,
    load_sem, y_send, y_recv, c_send, c_recv, g_send, g_recv, x_send, x_recv, yx_send, yx_recv,
    core_send, core_recv, chip_send, chip_recv,
):
    n_ep = x_full.shape[0]
    rows, model_width = q_ref.shape
    cap = x_comp.shape[3]
    half = model_width // 2
    width = weight_gate.shape[1]
    kv_heads = k_ref.shape[1] // HEAD_DIM
    group_size = model_width // k_ref.shape[1]
    block = model_width // 4
    scale = 1.0 / math.sqrt(HEAD_DIM)
    grp, expert, shard = lax.axis_index("grp"), lax.axis_index("ep"), lax.axis_index("sq")
    peer = 1 - shard
    last = n_ep - 1
    right, left = lax.rem(expert + 1, n_ep), lax.rem(expert + last, n_ep)
    inner = jnp.logical_and(expert > 0, expert < last)
    core = lax.rem(grp, 2)
    chip = grp // 2
    sibling = chip * 2 + 1 - core
    across = (1 - chip) * 2 + core
    diagonal = (1 - chip) * 2 + 1 - core
    peer_columns = pl.ds(pl.multiple_of(peer * width, width), width)
    own_columns = pl.ds(pl.multiple_of(shard * width, width), width)

    def load(i, src, dst):
        return pltpu.make_async_copy(src, dst, load_sem.at[i])

    loads = [
        load(0, q_hbm, q_ref),
        load(1, k_hbm, k_ref),
        load(2, v_hbm, v_ref),
        load(3, hidden_hbm.at[:, own_columns], g_full.at[expert, 0]),
        load(4, gate_hbm, weight_gate),
        load(5, up_hbm, weight_up),
    ]
    for copy in loads:
        copy.start()

    barrier = pltpu.get_barrier_semaphore()
    for target in ({"sq": peer}, {"ep": right}, {"ep": left}, {"grp": sibling}, {"grp": across}):
        pl.semaphore_signal(barrier, inc=1, device_id=target, device_id_type=MESH)
    pl.semaphore_wait(barrier, 5)

    def send(src, dst, send_sem, recv_sem, target):
        return pltpu.make_async_remote_copy(
            src_ref=src, dst_ref=dst, send_sem=send_sem, recv_sem=recv_sem,
            device_id=target, device_id_type=MESH,
        )

    def neighbour(d):
        return {"ep": right if d else left}

    def c_copy(z, j, d):
        return send(c_buf.at[z, j], c_buf.at[z, j], c_send.at[d, z, j], c_recv.at[z, j],
                    neighbour(d))

    def g_whole(z, j, d):
        return send(g_full.at[z, j], g_full.at[z, j], g_send.at[d, z, j], g_recv.at[z, j],
                    neighbour(d))

    def g_picked(z, j, d):
        return send(g_out.at[z, j], g_comp.at[z, j], g_send.at[d, z, j], g_recv.at[z, j],
                    neighbour(d))

    def x_whole(z, h, d):
        return send(x_full.at[z, h], x_full.at[z, h], x_send.at[d, z, h], x_recv.at[z, h],
                    neighbour(d))

    def x_picked(z, h, d):
        return send(x_out.at[z, h], x_comp.at[z, 0, h], x_send.at[d, z, h], x_recv.at[z, h],
                    neighbour(d))

    def yx(z, h):
        return send(x_comp.at[z, 0, h], x_comp.at[z, 1, h], yx_send.at[z, h], yx_recv.at[z, h],
                    {"sq": peer})

    def goes(d):
        return expert < last if d else expert > 0

    def to_inner(d):
        return expert < last - 1 if d else expert > 1

    def to_end(d):
        return expert == last - 1 if d else expert == 1

    def end_of(d):
        return last if d else 0

    y_keys = send(k_hbm, kv_buf.at[0], y_send.at[0], y_recv.at[0], {"sq": peer})
    y_values = send(v_hbm, kv_buf.at[1], y_send.at[1], y_recv.at[1], {"sq": peer})
    y_share = send(share_ref, c_buf.at[expert, 1], y_send.at[2], y_recv.at[2], {"sq": peer})
    y_grad = send(hidden_hbm.at[:, peer_columns], g_full.at[expert, 1],
                  y_send.at[3], y_recv.at[3], {"sq": peer})
    y_share.start()
    y_keys.start()
    y_values.start()
    y_grad.start()
    c_buf[expert, 0] = share_ref[...]
    acc[...] = jnp.zeros_like(acc)
    upper = (
        lax.broadcasted_iota(jnp.int32, (rows, rows), 0)
        <= lax.broadcasted_iota(jnp.int32, (rows, rows), 1)
    ).astype(jnp.float32).astype(jnp.bfloat16)
    places = lax.broadcasted_iota(jnp.int32, (cap, rows), 0).astype(jnp.float32)

    def pick(z, j, who):
        share = c_buf[z, j]
        here = lax.broadcasted_iota(jnp.int32, share.shape, 0) == who
        share = jnp.sum(jnp.where(here, share, 0.0), axis=0, keepdims=True)
        routed = jnp.where(share > 0.0, 1.0, 0.0)
        count = jnp.dot(
            jnp.broadcast_to(routed, (16, rows)).astype(jnp.bfloat16), upper,
            preferred_element_type=jnp.float32,
        )[:1]
        key = jnp.where(share > 0.0, count - 1.0, -1.0)
        return places == key, share

    def chooser(z, j, who):
        return jnp.where(pick(z, j, who)[0], 1.0, 0.0).astype(jnp.bfloat16)

    def picked(choice, array):
        return jnp.dot(choice, array, preferred_element_type=jnp.float32).astype(jnp.bfloat16)

    def pass_grad(z, j, d):
        @pl.when(goes(d))
        def _():
            c_copy(z, j, d).start()

        @pl.when(to_inner(d))
        def _():
            g_whole(z, j, d).start()

        @pl.when(to_end(d))
        def _():
            g_out[z, j] = picked(chooser(z, j, end_of(d)), g_full[z, j])
            g_picked(z, j, d).start()

    def pass_tokens(z, h, d):
        @pl.when(to_inner(d))
        def _():
            x_whole(z, h, d).start()

        @pl.when(to_end(d))
        def _():
            x_out[z, h] = picked(chooser(z, 0, end_of(d)), x_full[z, h])
            x_picked(z, h, d).start()

    def keep_tokens(z, h):
        x_comp[z, 0, h] = picked(chooser(z, 0, expert), x_full[z, h])
        yx(z, h).start()

    loads[3].wait()
    for d in range(2):
        pass_grad(expert, 0, d)
    for copy in loads[:3]:
        copy.wait()
    y_keys.wait_recv()
    y_values.wait_recv()

    contract = (((1,), (1,)), ((), ()))
    part_rows = rows // 2

    @pl.loop(0, 2)
    def _(p):
        part = pl.ds(pl.multiple_of(p * part_rows, part_rows), part_rows)
        causal = lax.broadcasted_iota(jnp.int32, (part_rows, rows), 1) <= (
            lax.broadcasted_iota(jnp.int32, (part_rows, rows), 0) + p * part_rows
        )
        seen = lax.broadcasted_iota(jnp.int32, (part_rows, rows), 1) < shard * rows
        squares = jnp.zeros((part_rows, 1), jnp.float32)
        for head in range(kv_heads * group_size):
            cols = slice(head * HEAD_DIM, (head + 1) * HEAD_DIM)
            kv = head // group_size
            kv_cols = slice(kv * HEAD_DIM, (kv + 1) * HEAD_DIM)
            q = q_ref[part, cols]
            own = lax.dot_general(
                q, k_ref[:, kv_cols], contract, preferred_element_type=jnp.float32
            )
            old = lax.dot_general(
                q, kv_buf[0, :, kv_cols], contract, preferred_element_type=jnp.float32
            )
            own = jnp.where(causal, own * scale, masked_score)
            old = jnp.where(seen, old * scale, masked_score)
            top = jnp.maximum(
                jnp.max(own, axis=1, keepdims=True), jnp.max(old, axis=1, keepdims=True)
            )
            own = jnp.exp(own - top)
            old = jnp.exp(old - top)
            total = jnp.sum(own, axis=1, keepdims=True) + jnp.sum(old, axis=1, keepdims=True)
            out = jnp.dot(
                own.astype(jnp.bfloat16), v_ref[:, kv_cols], preferred_element_type=jnp.float32
            ) + jnp.dot(
                old.astype(jnp.bfloat16), kv_buf[1, :, kv_cols],
                preferred_element_type=jnp.float32,
            )
            out = out / total
            attended[:, cols] = out
            squares = squares + jnp.sum(out * out, axis=1, keepdims=True)
        inverse = lax.rsqrt(squares / model_width + epsilon)
        normed = (attended[...] * inverse * gain_ref[...]).astype(jnp.bfloat16)
        x_full[expert, 0, part] = normed[:, :half]
        x_full[expert, 1, part] = normed[:, half:]

    for h in range(2):
        for d in range(2):
            pass_tokens(expert, h, d)
        keep_tokens(expert, h)
    y_share.wait_recv()
    y_grad.wait_recv()
    for d in range(2):
        pass_grad(expert, 1, d)
    for j in range(2):
        g_comp[expert, j] = picked(chooser(expert, j, expert), g_full[expert, j])
    for copy in loads[4:]:
        copy.wait()

    tile = min(256, width)

    def columns(b):
        return pl.ds(pl.multiple_of(b * block, block), block)

    def add_piece(z, j):
        where, share = pick(z, j, expert)
        share = jnp.sum(jnp.where(where, share, 0.0), axis=1, keepdims=True)

        @pl.loop(0, width // tile)
        def _(t):
            cols = pl.ds(pl.multiple_of(t * tile, tile), tile)

            def product(weight):
                return jnp.dot(
                    x_comp[z, j, 0], weight[:half, cols], preferred_element_type=jnp.float32
                ) + jnp.dot(
                    x_comp[z, j, 1], weight[half:, cols], preferred_element_type=jnp.float32
                )

            pre_gate = product(weight_gate)
            pre_up = product(weight_up)
            cotangent = (share * g_comp[z, j, :, cols].astype(jnp.float32)).astype(jnp.bfloat16)
            sigmoid_gate = 1.0 / (1.0 + jnp.exp(-pre_gate))
            slope = sigmoid_gate * (1.0 + pre_gate * (1.0 - sigmoid_gate))
            delta_ref[:, cols] = (cotangent.astype(jnp.float32) * pre_up * slope).astype(
                jnp.bfloat16
            )

        for h in range(2):

            @pl.loop(0, 2)
            def _(b):
                acc[:, columns(h * 2 + b)] += lax.dot_general(
                    delta_ref[...], x_comp[z, j, h, :, columns(b)], (((0,), (0,)), ((), ())),
                    preferred_element_type=jnp.float32,
                )

    def add_chunk(z):
        @pl.loop(0, 2)
        def _(j):
            @pl.when(j == 1)
            def _():
                yx(z, 0).wait_recv()
                yx(z, 1).wait_recv()

            add_piece(z, j)

    def present(z):
        return jnp.logical_and(z >= 0, z <= last)

    @pl.loop(1, n_ep + 1)
    def _(dist):
        for d in range(2):
            z = expert - dist if d else expert + dist

            @pl.when(present(z))
            def _():
                for j in range(2):
                    c_copy(z, j, d).wait_recv()

            @pl.when(jnp.logical_and(present(z), inner))
            def _():
                for j in range(2):
                    g_whole(z, j, d).wait_recv()
                    pass_grad(z, j, d)
                for h in range(2):
                    x_whole(z, h, d).wait_recv()
                    pass_tokens(z, h, d)
                    keep_tokens(z, h)
                for j in range(2):
                    g_comp[z, j] = picked(chooser(z, j, expert), g_full[z, j])

            @pl.when(jnp.logical_and(present(z), jnp.logical_not(inner)))
            def _():
                for j in range(2):
                    g_picked(z, j, d).wait_recv()
                for h in range(2):
                    x_picked(z, h, d).wait_recv()
                    yx(z, h).start()

        @pl.when(dist == 1)
        def _():
            add_chunk(expert)

        @pl.loop(0, 2)
        def _(d):
            z = expert + (dist - 1) * (1 - 2 * d)

            @pl.when(jnp.logical_and(dist > 1, present(z)))
            def _():
                add_chunk(z)

    def to_core(i):
        return send(stage.at[i], from_core.at[i], core_send.at[i], core_recv.at[i],
                    {"grp": sibling})

    to_chip = send(carry, from_chip, chip_send, chip_recv, {"grp": across})
    stage[0] = acc[:, columns(diagonal)].astype(jnp.bfloat16)
    to_core(0).start()
    stage[1] = acc[:, columns(sibling)].astype(jnp.bfloat16)
    to_core(0).wait_recv()
    carry[...] = (acc[:, columns(across)] + from_core[0].astype(jnp.float32)).astype(jnp.bfloat16)
    to_chip.start()
    to_core(1).start()
    to_core(1).wait_recv()
    acc[:, columns(grp)] += from_core[1].astype(jnp.float32)
    to_chip.wait_recv()
    out_ref[...] = (acc[:, columns(grp)] + from_chip[...].astype(jnp.float32)).T

    for copy in (y_keys, y_values, y_share, y_grad, to_core(0), to_core(1), to_chip):
        copy.wait_send()

    @pl.loop(0, n_ep)
    def _(z):
        for i in range(2):
            yx(z, i).wait_send()
            for d in range(2):
                passed = z <= expert if d else z >= expert

                @pl.when(jnp.logical_and(passed, goes(d)))
                def _():
                    c_copy(z, i, d).wait_send()

                @pl.when(jnp.logical_and(passed, to_inner(d)))
                def _():
                    g_whole(z, i, d).wait_send()
                    x_whole(z, i, d).wait_send()

                @pl.when(jnp.logical_and(passed, to_end(d)))
                def _():
                    g_picked(z, i, d).wait_send()
                    x_picked(z, i, d).wait_send()


def fused(
    queries, keys, values, norm_gain, expert_ids, gate_values, hidden_grad, gate_weight, up_weight
):
    rows, model_width = queries.shape
    n_ep = lax.axis_size("ep")
    width = gate_weight.shape[2]
    kv_width = keys.shape[1]
    block = model_width // 4
    half = model_width // 2
    cap = rows * expert_ids.shape[1] // n_ep * 3 // 2
    chosen = expert_ids.T[:, None, :] == jnp.arange(8, dtype=jnp.int32)[:, None]
    share = jnp.sum(jnp.where(chosen, gate_values.T[:, None, :], 0.0), axis=0)
    vmem = pl.BlockSpec(memory_space=pltpu.VMEM)
    hbm = pl.BlockSpec(memory_space=pltpu.HBM)
    dma = pltpu.SemaphoreType.DMA
    bf16, f32 = jnp.bfloat16, jnp.float32
    out = pl.pallas_call(
        whole_kernel,
        out_shape=jax.ShapeDtypeStruct((block, width), f32),
        in_specs=[hbm] * 3 + [vmem] * 2 + [hbm] * 3,
        out_specs=vmem,
        scratch_shapes=[
            pltpu.VMEM((rows, model_width), bf16),
            pltpu.VMEM((rows, kv_width), bf16),
            pltpu.VMEM((rows, kv_width), bf16),
            pltpu.VMEM((n_ep, 2, rows, half), bf16),
            pltpu.VMEM((n_ep, 2, 2, cap, half), bf16),
            pltpu.VMEM((n_ep, 2, cap, half), bf16),
            pltpu.VMEM((n_ep, 2, rows, width), bf16),
            pltpu.VMEM((n_ep, 2, cap, width), bf16),
            pltpu.VMEM((n_ep, 2, cap, width), bf16),
            pltpu.VMEM((n_ep, 2, 8, rows), f32),
            pltpu.VMEM((2, rows, kv_width), bf16),
            pltpu.VMEM((model_width, width), bf16),
            pltpu.VMEM((model_width, width), bf16),
            pltpu.VMEM((cap, width), bf16),
            pltpu.VMEM((rows // 2, model_width), f32),
            pltpu.VMEM((width, model_width), f32),
            pltpu.VMEM((2, width, block), bf16),
            pltpu.VMEM((2, width, block), bf16),
            pltpu.VMEM((width, block), bf16),
            pltpu.VMEM((width, block), bf16),
            dma((6,)), dma((4,)), dma((4,)),
            dma((2, n_ep, 2)), dma((n_ep, 2)), dma((2, n_ep, 2)), dma((n_ep, 2)),
            dma((2, n_ep, 2)), dma((n_ep, 2)), dma((n_ep, 2)), dma((n_ep, 2)),
            dma((2,)), dma((2,)), dma, dma,
        ],
        compiler_params=pltpu.CompilerParams(
            collective_id=0, has_side_effects=True, vmem_limit_bytes=56 << 20
        ),
    )(
        queries, keys, values, norm_gain.reshape(1, -1), share, hidden_grad,
        gate_weight[0], up_weight[0],
    )
    return out[None]


def solution(mesh):
    small = mesh.shape["grp"] == 4 and mesh.shape["sq"] == 2 and mesh.shape["ep"] == 4
    return jax.shard_map(
        fused if small else body,
        mesh=mesh,
        in_specs=(
            P(("grp", "ep", "sq"), None),
            P(("grp", "ep", "sq"), None),
            P(("grp", "ep", "sq"), None),
            P(),
            P(("grp", "ep", "sq"), None),
            P(("grp", "ep", "sq"), None),
            P(("grp", "ep", "sq"), None),
            P("ep", None, "sq"),
            P("ep", None, "sq"),
        ),
        out_specs=P("ep", "grp", "sq"),
        check_vma=False,
    )
```

```python
import functools
import math

import jax
import jax.numpy as jnp
from jax import lax
from jax.experimental import pallas as pl
from jax.experimental.pallas import tpu as pltpu
from jax.sharding import PartitionSpec as P

HEAD_DIM = 128

epsilon = 1e-05
masked_score = -1e30
MESH = pl.DeviceIdType.MESH


def attention_kernel(group_size, shard_ref, q_ref, ko_ref, vo_ref, kp_ref, vp_ref, gain_ref, out_ref, acc_ref):
    rows, model_width = q_ref.shape
    past = kp_ref.shape[0]
    scale = 1.0 / math.sqrt(HEAD_DIM)
    shard = shard_ref[0]
    contract = (((1,), (1,)), ((), ()))
    causal = lax.broadcasted_iota(jnp.int32, (rows, rows), 1) <= lax.broadcasted_iota(
        jnp.int32, (rows, rows), 0
    )
    seen = lax.broadcasted_iota(jnp.int32, (rows, past), 1) < shard * rows
    squares = jnp.zeros((rows, 1), jnp.float32)
    for head in range(model_width // HEAD_DIM):
        cols = slice(head * HEAD_DIM, (head + 1) * HEAD_DIM)
        kv = head // group_size
        kv_cols = slice(kv * HEAD_DIM, (kv + 1) * HEAD_DIM)
        q = q_ref[:, cols]
        own = lax.dot_general(q, ko_ref[:, kv_cols], contract, preferred_element_type=jnp.float32)
        old = lax.dot_general(q, kp_ref[:, kv_cols], contract, preferred_element_type=jnp.float32)
        own = jnp.where(causal, own * scale, masked_score)
        old = jnp.where(seen, old * scale, masked_score)
        top = jnp.maximum(
            jnp.max(own, axis=1, keepdims=True), jnp.max(old, axis=1, keepdims=True)
        )
        own = jnp.exp(own - top)
        old = jnp.exp(old - top)
        total = jnp.sum(own, axis=1, keepdims=True) + jnp.sum(old, axis=1, keepdims=True)
        out = jnp.dot(
            own.astype(jnp.bfloat16), vo_ref[:, kv_cols], preferred_element_type=jnp.float32
        ) + jnp.dot(
            old.astype(jnp.bfloat16), vp_ref[:, kv_cols], preferred_element_type=jnp.float32
        )
        out = out / total
        acc_ref[:, cols] = out
        squares = squares + jnp.sum(out * out, axis=1, keepdims=True)
    inverse = lax.rsqrt(squares / model_width + epsilon)
    out_ref[...] = (acc_ref[...] * inverse * gain_ref[...]).astype(jnp.bfloat16)


def attend(shard, queries, keys, values, past_keys, past_values, norm_gain):
    rows, model_width = queries.shape
    group_size = model_width // keys.shape[1]
    vmem = pl.BlockSpec(memory_space=pltpu.VMEM)
    return pl.pallas_call(
        functools.partial(attention_kernel, group_size),
        out_shape=jax.ShapeDtypeStruct((rows, model_width), jnp.bfloat16),
        in_specs=[pl.BlockSpec(memory_space=pltpu.SMEM)] + [vmem] * 6,
        out_specs=vmem,
        scratch_shapes=[pltpu.VMEM((rows, model_width), jnp.float32)],
        compiler_params=pltpu.CompilerParams(vmem_limit_bytes=32 << 20),
        cost_estimate=pl.CostEstimate(
            flops=4 * rows * model_width * (rows + past_keys.shape[0]),
            bytes_accessed=4 * rows * model_width,
            transcendentals=rows * (model_width // HEAD_DIM) * (rows + past_keys.shape[0]),
        ),
    )(shard.reshape(1), queries, keys, values, past_keys, past_values, norm_gain.reshape(1, -1))


def ring(size, shift):
    return [(i, (i + shift) % size) for i in range(size)]


def body(
    queries, keys, values, norm_gain, expert_ids, gate_values, hidden_grad, gate_weight, up_weight
):
    rows, model_width = queries.shape
    n_ep = lax.axis_size("ep")
    n_sq = lax.axis_size("sq")
    shard = lax.axis_index("sq")
    expert = lax.axis_index("ep")
    weight_gate = gate_weight[0]
    weight_up = up_weight[0]
    width = weight_gate.shape[1]
    kv_width = keys.shape[1]

    both = jnp.concatenate([keys, values], axis=1)
    past = []
    for j in range(1, n_sq):
        past.append(lax.ppermute(both, "sq", [(i, i + j) for i in range(n_sq - j)]))
    past = jnp.concatenate(past, axis=0)

    def columns_of(owner):
        return lax.dynamic_slice_in_dim(hidden_grad, owner * width, width, 1)

    grads = [columns_of(shard)]
    for j in range(1, n_sq):
        grads.append(lax.ppermute(columns_of((shard + j) % n_sq), "sq", ring(n_sq, j)))
    grad = jnp.concatenate(grads, axis=0)

    chosen = expert_ids[:, :, None] == jnp.arange(n_ep, dtype=jnp.int32)
    share = jnp.sum(jnp.where(chosen, gate_values[:, :, None], 0.0), axis=1).T
    shares = lax.all_gather(share, ("ep", "sq"), axis=0, tiled=False)
    shares = lax.dynamic_index_in_dim(shares, expert, 1, keepdims=False).reshape(n_ep, n_sq, rows)
    order = (shard - jnp.arange(n_sq)) % n_sq
    shares = jnp.take(shares, order, axis=1).reshape(n_ep, n_sq * rows)

    normed = attend(
        shard, queries, keys, values, past[:, :kv_width], past[:, kv_width:], norm_gain
    )

    def add_chunk(step, tokens, grad, summed):
        source = (expert - step) % n_ep
        share_here = lax.dynamic_index_in_dim(shares, source, 0, keepdims=False)
        pieces = [tokens]
        for j in range(1, n_sq):
            pieces.append(lax.ppermute(tokens, "sq", ring(n_sq, j)))
        for j, inputs in enumerate(pieces):
            part = slice(j * rows, (j + 1) * rows)
            cotangent = (share_here[part, None] * grad[part].astype(jnp.float32)).astype(
                jnp.bfloat16
            )
            pre_gate = jnp.dot(inputs, weight_gate, preferred_element_type=jnp.float32)
            pre_up = jnp.dot(inputs, weight_up, preferred_element_type=jnp.float32)
            sigmoid_gate = jax.nn.sigmoid(pre_gate)
            slope = sigmoid_gate * (1.0 + pre_gate * (1.0 - sigmoid_gate))
            delta = (cotangent.astype(jnp.float32) * pre_up * slope).astype(jnp.bfloat16)
            term = lax.dot_general(
                inputs, delta, (((0,), (0,)), ((), ())), preferred_element_type=jnp.float32
            )
            summed = term if summed is None else summed + term
        return summed

    def turn(tokens, grad):
        return lax.ppermute(tokens, "ep", ring(n_ep, 1)), lax.ppermute(grad, "ep", ring(n_ep, 1))

    if n_ep <= 8:
        summed = None
        tokens = normed
        for step in range(n_ep):
            if step < n_ep - 1:
                turned = turn(tokens, grad)
            summed = add_chunk(step, tokens, grad, summed)
            if step < n_ep - 1:
                tokens, grad = turned
    else:

        def one_step(step, carried):
            tokens, grad, summed = carried
            turned = turn(tokens, grad)
            return (*turned, add_chunk(step, tokens, grad, summed))

        start = jnp.zeros((model_width, width), jnp.float32)
        summed = lax.fori_loop(0, n_ep, one_step, (normed, grad, start))[2]
    return lax.psum_scatter(
        summed[None].astype(jnp.bfloat16), "grp", scatter_dimension=1, tiled=True
    ).astype(jnp.float32)


def whole_kernel(
    q_hbm, k_hbm, v_hbm, gain_ref, share_ref, hidden_hbm, gate_hbm, up_hbm, out_ref,
    q_ref, k_ref, v_ref, x_full, x_comp, x_out, g_full, g_comp, g_out, c_buf, kv_buf,
    weight_gate, weight_up, delta_ref, attended, acc, stage, from_core, carry, from_chip,
    load_sem, y_send, y_recv, c_send, c_recv, g_send, g_recv, x_send, x_recv, yx_send, yx_recv,
    core_send, core_recv, chip_send, chip_recv,
):
    n_ep = x_full.shape[0]
    rows, model_width = q_ref.shape
    cap = x_comp.shape[3]
    parts = x_full.shape[1]
    half = model_width // parts
    width = weight_gate.shape[1]
    kv_heads = k_ref.shape[1] // HEAD_DIM
    group_size = model_width // k_ref.shape[1]
    block = model_width // 4
    scale = 1.0 / math.sqrt(HEAD_DIM)
    grp, expert, shard = lax.axis_index("grp"), lax.axis_index("ep"), lax.axis_index("sq")
    peer = 1 - shard
    last = n_ep - 1
    right, left = lax.rem(expert + 1, n_ep), lax.rem(expert + last, n_ep)
    inner = jnp.logical_and(expert > 0, expert < last)
    core = lax.rem(grp, 2)
    chip = grp // 2
    sibling = chip * 2 + 1 - core
    across = (1 - chip) * 2 + core
    diagonal = (1 - chip) * 2 + 1 - core
    peer_columns = pl.ds(pl.multiple_of(peer * width, width), width)
    own_columns = pl.ds(pl.multiple_of(shard * width, width), width)

    def load(i, src, dst):
        return pltpu.make_async_copy(src, dst, load_sem.at[i])

    loads = [
        load(0, q_hbm, q_ref),
        load(1, k_hbm, k_ref),
        load(2, v_hbm, v_ref),
        load(3, hidden_hbm.at[:, own_columns], g_full.at[expert, 0]),
        load(4, gate_hbm, weight_gate),
        load(5, up_hbm, weight_up),
    ]
    for copy in loads:
        copy.start()

    barrier = pltpu.get_barrier_semaphore()
    for target in ({"sq": peer}, {"ep": right}, {"ep": left}, {"grp": sibling}, {"grp": across}):
        pl.semaphore_signal(barrier, inc=1, device_id=target, device_id_type=MESH)
    pl.semaphore_wait(barrier, 5)

    def send(src, dst, send_sem, recv_sem, target):
        return pltpu.make_async_remote_copy(
            src_ref=src, dst_ref=dst, send_sem=send_sem, recv_sem=recv_sem,
            device_id=target, device_id_type=MESH,
        )

    def neighbour(d):
        return {"ep": right if d else left}

    def c_copy(z, j, d):
        return send(c_buf.at[z, j], c_buf.at[z, j], c_send.at[d, z, j], c_recv.at[z, j],
                    neighbour(d))

    def g_whole(z, j, d):
        return send(g_full.at[z, j], g_full.at[z, j], g_send.at[d, z, j], g_recv.at[z, j],
                    neighbour(d))

    def g_picked(z, j, d):
        return send(g_out.at[z, j], g_comp.at[z, j], g_send.at[d, z, j], g_recv.at[z, j],
                    neighbour(d))

    def x_whole(z, h, d):
        return send(x_full.at[z, h], x_full.at[z, h], x_send.at[d, z, h], x_recv.at[z, h],
                    neighbour(d))

    def x_picked(z, h, d):
        return send(x_out.at[z, h], x_comp.at[z, 0, h], x_send.at[d, z, h], x_recv.at[z, h],
                    neighbour(d))

    def yx(z, h):
        return send(x_comp.at[z, 0, h], x_comp.at[z, 1, h], yx_send.at[z, h], yx_recv.at[z, h],
                    {"sq": peer})

    def goes(d):
        return expert < last if d else expert > 0

    def to_inner(d):
        return expert < last - 1 if d else expert > 1

    def to_end(d):
        return expert == last - 1 if d else expert == 1

    def end_of(d):
        return last if d else 0

    y_keys = send(k_hbm, kv_buf.at[0], y_send.at[0], y_recv.at[0], {"sq": peer})
    y_values = send(v_hbm, kv_buf.at[1], y_send.at[1], y_recv.at[1], {"sq": peer})
    y_share = send(share_ref, c_buf.at[expert, 1], y_send.at[2], y_recv.at[2], {"sq": peer})
    y_grad = send(hidden_hbm.at[:, peer_columns], g_full.at[expert, 1],
                  y_send.at[3], y_recv.at[3], {"sq": peer})
    y_share.start()
    y_keys.start()
    y_values.start()
    y_grad.start()
    c_buf[expert, 0] = share_ref[...]
    acc[...] = jnp.zeros_like(acc)
    upper = (
        lax.broadcasted_iota(jnp.int32, (rows, rows), 0)
        <= lax.broadcasted_iota(jnp.int32, (rows, rows), 1)
    ).astype(jnp.float32).astype(jnp.bfloat16)
    places = lax.broadcasted_iota(jnp.int32, (cap, rows), 0).astype(jnp.float32)

    def pick(z, j, who):
        share = c_buf[z, j]
        here = lax.broadcasted_iota(jnp.int32, share.shape, 0) == who
        share = jnp.sum(jnp.where(here, share, 0.0), axis=0, keepdims=True)
        routed = jnp.where(share > 0.0, 1.0, 0.0)
        count = jnp.dot(
            jnp.broadcast_to(routed, (16, rows)).astype(jnp.bfloat16), upper,
            preferred_element_type=jnp.float32,
        )[:1]
        key = jnp.where(share > 0.0, count - 1.0, -1.0)
        return places == key, share

    def chooser(z, j, who):
        return jnp.where(pick(z, j, who)[0], 1.0, 0.0).astype(jnp.bfloat16)

    def picked(choice, array):
        return jnp.dot(choice, array, preferred_element_type=jnp.float32).astype(jnp.bfloat16)

    def pass_grad(z, j, d):
        @pl.when(goes(d))
        def _():
            c_copy(z, j, d).start()

        @pl.when(to_inner(d))
        def _():
            g_whole(z, j, d).start()

        @pl.when(to_end(d))
        def _():
            g_out[z, j] = picked(chooser(z, j, end_of(d)), g_full[z, j])
            g_picked(z, j, d).start()

    def pass_tokens(z, h, d):
        @pl.when(to_inner(d))
        def _():
            x_whole(z, h, d).start()

        @pl.when(to_end(d))
        def _():
            x_out[z, h] = picked(chooser(z, 0, end_of(d)), x_full[z, h])
            x_picked(z, h, d).start()

    def keep_tokens(z, h):
        x_comp[z, 0, h] = picked(chooser(z, 0, expert), x_full[z, h])
        yx(z, h).start()

    loads[3].wait()
    for d in range(2):
        pass_grad(expert, 0, d)
    for copy in loads[:3]:
        copy.wait()
    y_keys.wait_recv()
    y_values.wait_recv()

    contract = (((1,), (1,)), ((), ()))
    part_rows = rows // 2

    @pl.loop(0, 2)
    def _(p):
        part = pl.ds(pl.multiple_of(p * part_rows, part_rows), part_rows)
        causal = lax.broadcasted_iota(jnp.int32, (part_rows, rows), 1) <= (
            lax.broadcasted_iota(jnp.int32, (part_rows, rows), 0) + p * part_rows
        )
        seen = lax.broadcasted_iota(jnp.int32, (part_rows, rows), 1) < shard * rows
        squares = jnp.zeros((part_rows, 1), jnp.float32)
        for head in range(kv_heads * group_size):
            cols = slice(head * HEAD_DIM, (head + 1) * HEAD_DIM)
            kv = head // group_size
            kv_cols = slice(kv * HEAD_DIM, (kv + 1) * HEAD_DIM)
            q = q_ref[part, cols]
            own = lax.dot_general(
                q, k_ref[:, kv_cols], contract, preferred_element_type=jnp.float32
            )
            old = lax.dot_general(
                q, kv_buf[0, :, kv_cols], contract, preferred_element_type=jnp.float32
            )
            own = jnp.where(causal, own * scale, masked_score)
            old = jnp.where(seen, old * scale, masked_score)
            top = jnp.maximum(
                jnp.max(own, axis=1, keepdims=True), jnp.max(old, axis=1, keepdims=True)
            )
            own = jnp.exp(own - top)
            old = jnp.exp(old - top)
            total = jnp.sum(own, axis=1, keepdims=True) + jnp.sum(old, axis=1, keepdims=True)
            out = jnp.dot(
                own.astype(jnp.bfloat16), v_ref[:, kv_cols], preferred_element_type=jnp.float32
            ) + jnp.dot(
                old.astype(jnp.bfloat16), kv_buf[1, :, kv_cols],
                preferred_element_type=jnp.float32,
            )
            out = out / total
            attended[:, cols] = out
            squares = squares + jnp.sum(out * out, axis=1, keepdims=True)
        inverse = lax.rsqrt(squares / model_width + epsilon)
        normed = (attended[...] * inverse * gain_ref[...]).astype(jnp.bfloat16)
        for h in range(parts):
            x_full[expert, h, part] = normed[:, h * half : (h + 1) * half]

        @pl.when(p == 0)
        def _():
            y_share.wait_recv()
            y_grad.wait_recv()
            for d in range(2):
                pass_grad(expert, 1, d)

    for h in range(parts):
        for d in range(2):
            pass_tokens(expert, h, d)
        keep_tokens(expert, h)
    for j in range(2):
        g_comp[expert, j] = picked(chooser(expert, j, expert), g_full[expert, j])
    for copy in loads[4:]:
        copy.wait()

    tile = min(256, width)

    def columns(b):
        return pl.ds(pl.multiple_of(b * block, block), block)

    def add_piece(z, j):
        where, share = pick(z, j, expert)
        share = jnp.sum(jnp.where(where, share, 0.0), axis=1, keepdims=True)

        @pl.loop(0, width // tile)
        def _(t):
            cols = pl.ds(pl.multiple_of(t * tile, tile), tile)

            def product(weight):
                return sum(
                    jnp.dot(
                        x_comp[z, j, h], weight[h * half : (h + 1) * half, cols],
                        preferred_element_type=jnp.float32,
                    )
                    for h in range(parts)
                )

            pre_gate = product(weight_gate)
            pre_up = product(weight_up)
            cotangent = (share * g_comp[z, j, :, cols].astype(jnp.float32)).astype(jnp.bfloat16)
            sigmoid_gate = 1.0 / (1.0 + jnp.exp(-pre_gate))
            slope = sigmoid_gate * (1.0 + pre_gate * (1.0 - sigmoid_gate))
            delta_ref[:, cols] = (cotangent.astype(jnp.float32) * pre_up * slope).astype(
                jnp.bfloat16
            )

        @pl.loop(0, 4)
        def _(b):
            acc[:, columns(b)] += lax.dot_general(
                delta_ref[...], x_comp[z, j, b], (((0,), (0,)), ((), ())),
                preferred_element_type=jnp.float32,
            )

    def add_chunk(z):
        @pl.loop(0, 2)
        def _(j):
            @pl.when(j == 1)
            def _():
                for h in range(parts):
                    yx(z, h).wait_recv()

            add_piece(z, j)

    def present(z):
        return jnp.logical_and(z >= 0, z <= last)

    @pl.loop(1, n_ep + 1)
    def _(dist):
        for d in range(2):
            z = expert - dist if d else expert + dist

            @pl.when(present(z))
            def _():
                for j in range(2):
                    c_copy(z, j, d).wait_recv()

            @pl.when(jnp.logical_and(present(z), inner))
            def _():
                for j in range(2):
                    g_whole(z, j, d).wait_recv()
                    pass_grad(z, j, d)
                for h in range(parts):
                    x_whole(z, h, d).wait_recv()
                    pass_tokens(z, h, d)
                    keep_tokens(z, h)
                for j in range(2):
                    g_comp[z, j] = picked(chooser(z, j, expert), g_full[z, j])

            @pl.when(jnp.logical_and(present(z), jnp.logical_not(inner)))
            def _():
                for j in range(2):
                    g_picked(z, j, d).wait_recv()
                for h in range(parts):
                    x_picked(z, h, d).wait_recv()
                    yx(z, h).start()

        @pl.when(dist == 1)
        def _():
            add_chunk(expert)

        @pl.loop(0, 2)
        def _(d):
            z = expert + (dist - 1) * (1 - 2 * d)

            @pl.when(jnp.logical_and(dist > 1, present(z)))
            def _():
                add_chunk(z)

    slab = width // 2

    def to_core(i, t):
        rows_of = pl.ds(t * slab, slab)
        return send(stage.at[i, rows_of], from_core.at[i, rows_of], core_send.at[i, t],
                    core_recv.at[i, t], {"grp": sibling})

    def to_chip(t):
        rows_of = pl.ds(t * slab, slab)
        return send(carry.at[rows_of], from_chip.at[rows_of], chip_send.at[t], chip_recv.at[t],
                    {"grp": across})

    slabs = [slice(0, slab), slice(slab, width)]
    for t in range(2):
        stage[0, slabs[t]] = acc[slabs[t], columns(diagonal)].astype(jnp.bfloat16)
        to_core(0, t).start()
    for t in range(2):
        to_core(0, t).wait_recv()
        carry[slabs[t]] = (
            acc[slabs[t], columns(across)] + from_core[0, slabs[t]].astype(jnp.float32)
        ).astype(jnp.bfloat16)
        to_chip(t).start()
    for t in range(2):
        stage[1, slabs[t]] = acc[slabs[t], columns(sibling)].astype(jnp.bfloat16)
        to_core(1, t).start()
    for t in range(2):
        to_core(1, t).wait_recv()
        acc[slabs[t], columns(grp)] += from_core[1, slabs[t]].astype(jnp.float32)
    for t in range(2):
        to_chip(t).wait_recv()
        out_ref[:, slabs[t]] = (
            acc[slabs[t], columns(grp)] + from_chip[slabs[t]].astype(jnp.float32)
        ).T

    for copy in (y_keys, y_values, y_share, y_grad):
        copy.wait_send()
    for t in range(2):
        to_core(0, t).wait_send()
        to_core(1, t).wait_send()
        to_chip(t).wait_send()

    @pl.loop(0, n_ep)
    def _(z):
        for h in range(parts):
            yx(z, h).wait_send()
            for d in range(2):
                passed = z <= expert if d else z >= expert

                @pl.when(jnp.logical_and(passed, to_inner(d)))
                def _():
                    x_whole(z, h, d).wait_send()

                @pl.when(jnp.logical_and(passed, to_end(d)))
                def _():
                    x_picked(z, h, d).wait_send()

        for j in range(2):
            for d in range(2):
                passed = z <= expert if d else z >= expert

                @pl.when(jnp.logical_and(passed, goes(d)))
                def _():
                    c_copy(z, j, d).wait_send()

                @pl.when(jnp.logical_and(passed, to_inner(d)))
                def _():
                    g_whole(z, j, d).wait_send()

                @pl.when(jnp.logical_and(passed, to_end(d)))
                def _():
                    g_picked(z, j, d).wait_send()


def fused(
    queries, keys, values, norm_gain, expert_ids, gate_values, hidden_grad, gate_weight, up_weight
):
    rows, model_width = queries.shape
    n_ep = lax.axis_size("ep")
    width = gate_weight.shape[2]
    kv_width = keys.shape[1]
    block = model_width // 4
    parts = 4
    half = model_width // parts
    cap = rows * expert_ids.shape[1] // n_ep * 3 // 2
    chosen = expert_ids.T[:, None, :] == jnp.arange(8, dtype=jnp.int32)[:, None]
    share = jnp.sum(jnp.where(chosen, gate_values.T[:, None, :], 0.0), axis=0)
    vmem = pl.BlockSpec(memory_space=pltpu.VMEM)
    hbm = pl.BlockSpec(memory_space=pltpu.HBM)
    dma = pltpu.SemaphoreType.DMA
    bf16, f32 = jnp.bfloat16, jnp.float32
    out = pl.pallas_call(
        whole_kernel,
        out_shape=jax.ShapeDtypeStruct((block, width), f32),
        in_specs=[hbm] * 3 + [vmem] * 2 + [hbm] * 3,
        out_specs=vmem,
        scratch_shapes=[
            pltpu.VMEM((rows, model_width), bf16),
            pltpu.VMEM((rows, kv_width), bf16),
            pltpu.VMEM((rows, kv_width), bf16),
            pltpu.VMEM((n_ep, parts, rows, half), bf16),
            pltpu.VMEM((n_ep, 2, parts, cap, half), bf16),
            pltpu.VMEM((n_ep, parts, cap, half), bf16),
            pltpu.VMEM((n_ep, 2, rows, width), bf16),
            pltpu.VMEM((n_ep, 2, cap, width), bf16),
            pltpu.VMEM((n_ep, 2, cap, width), bf16),
            pltpu.VMEM((n_ep, 2, 8, rows), f32),
            pltpu.VMEM((2, rows, kv_width), bf16),
            pltpu.VMEM((model_width, width), bf16),
            pltpu.VMEM((model_width, width), bf16),
            pltpu.VMEM((cap, width), bf16),
            pltpu.VMEM((rows // 2, model_width), f32),
            pltpu.VMEM((width, model_width), f32),
            pltpu.VMEM((2, width, block), bf16),
            pltpu.VMEM((2, width, block), bf16),
            pltpu.VMEM((width, block), bf16),
            pltpu.VMEM((width, block), bf16),
            dma((6,)), dma((4,)), dma((4,)),
            dma((2, n_ep, 2)), dma((n_ep, 2)), dma((2, n_ep, 2)), dma((n_ep, 2)),
            dma((2, n_ep, parts)), dma((n_ep, parts)), dma((n_ep, parts)), dma((n_ep, parts)),
            dma((2, 2)), dma((2, 2)), dma((2,)), dma((2,)),
        ],
        compiler_params=pltpu.CompilerParams(
            collective_id=0, has_side_effects=True, vmem_limit_bytes=56 << 20
        ),
    )(
        queries, keys, values, norm_gain.reshape(1, -1), share, hidden_grad,
        gate_weight[0], up_weight[0],
    )
    return out[None]


def solution(mesh):
    small = mesh.shape["grp"] == 4 and mesh.shape["sq"] == 2 and mesh.shape["ep"] == 4
    return jax.shard_map(
        fused if small else body,
        mesh=mesh,
        in_specs=(
            P(("grp", "ep", "sq"), None),
            P(("grp", "ep", "sq"), None),
            P(("grp", "ep", "sq"), None),
            P(),
            P(("grp", "ep", "sq"), None),
            P(("grp", "ep", "sq"), None),
            P(("grp", "ep", "sq"), None),
            P("ep", None, "sq"),
            P("ep", None, "sq"),
        ),
        out_specs=P("ep", "grp", "sq"),
        check_vma=False,
    )
```
